32 devices in a mesh: req: 4 (over x, core), mlp: 8 (over z, y).
Axes of the slice: x: 2, y: 2, z: 4, core: 2. Of those that a mesh axis runs over, the one named last changes fastest.
Arguments:
- resid: bfloat16 [4096, 3072], P(('req', 'mlp')), may hold values from -6 to 6
- queries: bfloat16 [4096, 1536], P(('req', 'mlp')), may hold values from -240 to 240
- fresh_keys: bfloat16 [4096, 256], P(('req', 'mlp')), may hold values from -6 to 6
- fresh_values: bfloat16 [4096, 256], P(('req', 'mlp')), may hold values from -6 to 6
- paged_key_cache: bfloat16 [64, 128, 256], P(('req', 'mlp')), may hold values from -6 to 6
- paged_value_cache: bfloat16 [64, 128, 256], P(('req', 'mlp')), may hold values from -6 to 6
- page_table: int32 [4, 16], P('req'), may hold values from 0 to 15, as said below
- cache_lengths: int32 [4], P('req'), may hold values from 1 to 2048, as said below
- out_weight: bfloat16 [1536, 3072], replicated, may hold values from -0.15625 to 0.15625
- norm_gain: float32 [3072], replicated, may hold values from 0.5 to 1.5
- gate_weight: bfloat16 [3072, 8192], P('req', 'mlp'), may hold values from -0.109375 to 0.109375
- up_weight: bfloat16 [3072, 8192], P('req', 'mlp'), may hold values from -0.109375 to 0.109375
- down_weight: bfloat16 [8192, 3072], P('mlp', 'req'), may hold values from -0.0625 to 0.0625
Outputs:
- layer_out: bfloat16 [4096, 3072], P(('req', 'mlp'))
The draws below stay inside these ranges and needn't reach their ends.
Inputs may be any that keep to these rules, and one draw needn't show every extreme that they name: `page_table`: within the 1 request of one index of req the entries are a permutation of 0 to 15. `cache_lengths`: half of the requests hold at most 128 cached tokens, the other half more than 1920; some request holds exactly 2048.
All inputs are finite; a program needn't handle non-finite values.
Results may differ from the reference program's by a relative error of at most 0.0085.
Values may be sent and summed in bfloat16 or wider, within the bound.
A program may use at most 128 MiB of HBM per device.

```python
import jax
import jax.numpy as jnp
from jax import lax

D = 3072
QUERY_HEADS = 12
KEY_VALUE_HEADS = 2
HEAD_SIZE = 128
FF = 8192
REQ_DEV = 1
PAGE_TOKENS = 128
PAGES = 16
NEW_TOKENS = 1024
REQUEST_COUNT = 4
TOKEN_COUNT = 4096
CONTEXT_LIMIT = 2048
GROUP_SLOTS = 16
POOL_PAGES = 64
N_MLP = 8


def draw_queries(key, part):
    base = jnp.clip(jax.random.normal(key, (TOKEN_COUNT, QUERY_HEADS * HEAD_SIZE), jnp.float32), -6.0, 6.0)
    return base.astype(jnp.bfloat16)


def draw_page_table(key, part):
    blocks = REQUEST_COUNT // REQ_DEV
    joined_keys = jax.random.split(jax.random.fold_in(key, 11), blocks)
    orders = jax.vmap(lambda k: jax.random.permutation(k, GROUP_SLOTS))(joined_keys)
    return orders.reshape(REQUEST_COUNT, PAGES).astype(jnp.int32)


def draw_cache_lengths(key, part):
    order = jax.random.permutation(jax.random.fold_in(key, 21), REQUEST_COUNT).astype(jnp.int32)
    longer = CONTEXT_LIMIT - jax.random.randint(jax.random.fold_in(key, 22), (REQUEST_COUNT,), 0, PAGE_TOKENS)
    shorter = jax.random.randint(jax.random.fold_in(key, 23), (REQUEST_COUNT,), 1, PAGE_TOKENS + 1)
    lengths = jnp.where(order < REQUEST_COUNT // 2, longer, shorter)
    lengths = jnp.where(order == 0, CONTEXT_LIMIT, lengths)
    return lengths.astype(jnp.int32)


def shard_levels(key, extent, cuts, least, high):
    def one(position, parts):
        heights = jax.random.uniform(jax.random.fold_in(jax.random.fold_in(key, 6), position), (parts,), jnp.float32, least / len(cuts), high / len(cuts))
        return jnp.repeat(jnp.exp(heights), extent[position] // parts).reshape((-1,) + (1,) * (len(extent) - position - 1))

    gain = one(*cuts[0])
    for cut in cuts[1:]:
        gain = gain * one(*cut)
    return gain


def noise(key, shape, scale, most, cuts=(), kind=jnp.bfloat16):
    factor_of = shard_levels(key, shape, cuts, -0.22, 0.18) if cuts else 1.0
    entries = jax.random.normal(key, shape, jnp.float32) * scale * factor_of
    return jnp.minimum(jnp.maximum(entries, -most), most).astype(kind)


def setup_inputs(seed: int = 0) -> dict:
    seeds = jax.random.split(jax.random.key(seed), 14)
    resid = noise(seeds[0], (TOKEN_COUNT, D), 1.0, 6.0, ((0, 32),))
    queries = draw_queries(jax.random.fold_in(seeds[13], 71), 0)
    fresh_keys = noise(seeds[2], (TOKEN_COUNT, KEY_VALUE_HEADS * HEAD_SIZE), 1.0, 6.0, ((0, 32),))
    fresh_values = noise(seeds[3], (TOKEN_COUNT, KEY_VALUE_HEADS * HEAD_SIZE), 1.0, 6.0, ((0, 32),))
    paged_key_cache = noise(seeds[4], (POOL_PAGES, PAGE_TOKENS, KEY_VALUE_HEADS * HEAD_SIZE), 1.0, 6.0, ((0, 32),))
    paged_value_cache = noise(seeds[5], (POOL_PAGES, PAGE_TOKENS, KEY_VALUE_HEADS * HEAD_SIZE), 1.0, 6.0, ((0, 32),))
    page_table = draw_page_table(jax.random.fold_in(seeds[13], 71), 0)
    cache_lengths = draw_cache_lengths(jax.random.fold_in(seeds[13], 71), 0)
    out_weight = noise(seeds[8], (QUERY_HEADS * HEAD_SIZE, D), (QUERY_HEADS * HEAD_SIZE) ** -0.5, 0.15625)
    norm_gain = jnp.clip(1.0 + 0.1 * jax.random.normal(seeds[9], (D,), jnp.float32), 0.5, 1.5)
    gate_weight = noise(seeds[10], (D, FF), D ** -0.5, 0.109375, ((0, 4), (1, 8)))
    up_weight = noise(seeds[11], (D, FF), D ** -0.5, 0.109375, ((0, 4), (1, 8)))
    down_weight = noise(seeds[12], (FF, D), FF ** -0.5, 0.0625, ((0, 8), (1, 4)))
    return {"resid": resid, "queries": queries, "fresh_keys": fresh_keys, "fresh_values": fresh_values, "paged_key_cache": paged_key_cache, "paged_value_cache": paged_value_cache, "page_table": page_table, "cache_lengths": cache_lengths, "out_weight": out_weight, "norm_gain": norm_gain, "gate_weight": gate_weight, "up_weight": up_weight, "down_weight": down_weight}


def attend_request(rows_of_queries, rows_of_keys, rows_of_values, table_row, length, request, paged_key_cache, paged_value_cache):
    group_ratio = QUERY_HEADS // KEY_VALUE_HEADS
    block = request // REQ_DEV
    cache_positions = (table_row + block * GROUP_SLOTS).astype(jnp.int32)
    stored_keys = jnp.take(paged_key_cache, cache_positions, axis=0).reshape(CONTEXT_LIMIT, KEY_VALUE_HEADS * HEAD_SIZE)
    stored_values = jnp.take(paged_value_cache, cache_positions, axis=0).reshape(CONTEXT_LIMIT, KEY_VALUE_HEADS * HEAD_SIZE)
    joined_keys = jnp.concatenate([stored_keys, rows_of_keys], axis=0).astype(jnp.float32).reshape(CONTEXT_LIMIT + NEW_TOKENS, KEY_VALUE_HEADS, HEAD_SIZE)
    joined_values = jnp.concatenate([stored_values, rows_of_values], axis=0).astype(jnp.float32).reshape(CONTEXT_LIMIT + NEW_TOKENS, KEY_VALUE_HEADS, HEAD_SIZE)
    heads_of_queries = rows_of_queries.astype(jnp.float32).reshape(NEW_TOKENS, KEY_VALUE_HEADS, group_ratio, HEAD_SIZE)
    scores = jnp.einsum('tgrd,kgd->grtk', heads_of_queries, joined_keys) * HEAD_SIZE ** (-0.5)
    columns = jnp.arange(CONTEXT_LIMIT + NEW_TOKENS, dtype=jnp.int32)
    rows = jnp.arange(NEW_TOKENS, dtype=jnp.int32)
    mask = jnp.where(columns[None, :] < CONTEXT_LIMIT, (columns < length)[None, :], columns[None, :] - CONTEXT_LIMIT <= rows[:, None])
    scores = jnp.where(mask, scores, -1e+30)
    peak = lax.optimization_barrier(jnp.max(scores, axis=-1, keepdims=True))
    expo = jnp.where(mask, jnp.exp(scores - peak), 0.0)
    total = lax.optimization_barrier(jnp.sum(expo, axis=-1))
    rounded = lax.optimization_barrier(expo.astype(jnp.bfloat16)).astype(jnp.float32)
    summed = jnp.einsum('grtk,kgd->grtd', rounded, joined_values) / total[..., None]
    return jnp.transpose(summed, (2, 0, 1, 3)).reshape(NEW_TOKENS, QUERY_HEADS * HEAD_SIZE).astype(jnp.bfloat16)

def reference(resid, queries, fresh_keys, fresh_values, paged_key_cache, paged_value_cache, page_table, cache_lengths, out_weight, norm_gain, gate_weight, up_weight, down_weight):
    query_sets = queries.reshape(REQUEST_COUNT, NEW_TOKENS, QUERY_HEADS * HEAD_SIZE)
    grouped_keys = fresh_keys.reshape(REQUEST_COUNT, NEW_TOKENS, KEY_VALUE_HEADS * HEAD_SIZE)
    grouped_values = fresh_values.reshape(REQUEST_COUNT, NEW_TOKENS, KEY_VALUE_HEADS * HEAD_SIZE)
    numbers = jnp.arange(REQUEST_COUNT, dtype=jnp.int32)

    def one(items):
        return attend_request(items[0], items[1], items[2], items[3], items[4], items[5], paged_key_cache, paged_value_cache)
    attn = lax.map(one, (query_sets, grouped_keys, grouped_values, page_table, cache_lengths, numbers)).reshape(TOKEN_COUNT, QUERY_HEADS * HEAD_SIZE)
    h = resid.astype(jnp.float32) + jnp.dot(attn, out_weight, preferred_element_type=jnp.float32)
    normed = (h * lax.rsqrt(lax.optimization_barrier(jnp.mean(h * h, axis=-1, keepdims=True)) + 1e-05) * norm_gain).astype(jnp.bfloat16)
    width_block = FF // N_MLP

    def add_block(index, total):
        start = index * width_block
        gate = jnp.dot(normed, lax.dynamic_slice_in_dim(gate_weight, start, width_block, 1), preferred_element_type=jnp.float32)
        upper = jnp.dot(normed, lax.dynamic_slice_in_dim(up_weight, start, width_block, 1), preferred_element_type=jnp.float32)
        hidden = (jax.nn.silu(gate) * upper).astype(jnp.bfloat16)
        partial_value = jnp.dot(hidden, lax.dynamic_slice_in_dim(down_weight, start, width_block, 0), preferred_element_type=jnp.float32)
        return total + lax.optimization_barrier(partial_value.astype(jnp.bfloat16)).astype(jnp.float32)
    summed = lax.fori_loop(0, N_MLP, add_block, jnp.zeros((TOKEN_COUNT, D), jnp.float32))
    return (h + summed).astype(jnp.bfloat16)
```

```python
import functools
import math

import jax
import jax.numpy as jnp
from jax import lax
from jax.experimental import pallas as pl
from jax.experimental.pallas import tpu as pltpu
from jax.sharding import PartitionSpec as P

QUERY_HEADS = 12
KEY_VALUE_HEADS = 2
HEAD_SIZE = 128
GROUP = QUERY_HEADS // KEY_VALUE_HEADS
KV_COLS = KEY_VALUE_HEADS * HEAD_SIZE
MESH = pl.DeviceIdType.MESH


def flip(a, k):
    bit = 1
    while bit <= k:
        if k & bit:
            a = a + bit - 2 * bit * (lax.rem(a // bit, 2))
        bit *= 2
    return a


def kernel(
    n, nr,
    q_ref, resid_ref, pos_ref, gain_ref, fk, fv, pk, pv, ow, wg, wu, wd,
    out_ref,
    kv, nrm, wgs, wus, wds, big, yrecv, zrecv, h, attn, bias, hid,
    loc, kv_send, kv_fwd, kv_recv, n_send, n_fwd, n_recv,
    w_send, w_fwd, w_recv, y_send, y_recv, z_send, z_recv,
):
    A, X = n // 2, nr // 2
    me, r = lax.axis_index("mlp"), lax.axis_index("req")
    a, b = me // 2, lax.rem(me, 2)
    x, c = r // 2, lax.rem(r, 2)
    partner, sibling = a * 2 + 1 - b, x * 2 + 1 - c
    T, D = resid_ref.shape
    cached = pk.shape[0]
    R = cached + T
    depth = wg.shape[0]
    F = wg.shape[1]
    Dq = wd.shape[1]

    def peer(k):
        return flip(a, k) * 2 + b

    def rpeer(k):
        return flip(x, k) * 2 + c

    def remote(src, dst, ss, rs, axis, idx):
        return pltpu.make_async_remote_copy(
            src_ref=src, dst_ref=dst, send_sem=ss, recv_sem=rs,
            device_id={axis: idx}, device_id_type=MESH,
        )

    def kv_slot(s):
        return kv.at[pl.ds(pl.multiple_of(s * R, 128), R), :]

    def n_slot(s):
        return nrm.at[pl.ds(pl.multiple_of(s * T, 128), T), :]

    def w_slot(i, s):
        if i == 2:
            return wds.at[s]
        buf = wgs if i == 0 else wus
        return buf.at[pl.ds(pl.multiple_of(s * depth, 128), depth), :]

    weights = (wg, wu, wd)

    base = pl.multiple_of(me * R, 128)
    mine = [
        pltpu.make_async_copy(pk, kv.at[pl.ds(base, cached), pl.ds(0, KV_COLS)], loc.at[0]),
        pltpu.make_async_copy(pv, kv.at[pl.ds(base, cached), pl.ds(KV_COLS, KV_COLS)], loc.at[1]),
        pltpu.make_async_copy(fk, kv.at[pl.ds(base + cached, T), pl.ds(0, KV_COLS)], loc.at[2]),
        pltpu.make_async_copy(fv, kv.at[pl.ds(base + cached, T), pl.ds(KV_COLS, KV_COLS)], loc.at[3]),
    ]
    own_ow = pltpu.make_async_copy(ow, big.at[pl.ds(0, ow.shape[0]), :], loc.at[4])
    own_w = [pltpu.make_async_copy(weights[i], w_slot(i, r), loc.at[5 + i]) for i in range(3)]
    for copy in mine:
        copy.start()

    barrier = pltpu.get_barrier_semaphore()
    pl.semaphore_signal(barrier, inc=1, device_id={"mlp": partner}, device_id_type=MESH)
    pl.semaphore_signal(barrier, inc=1, device_id={"req": sibling}, device_id_type=MESH)
    for k in range(1, A):
        pl.semaphore_signal(barrier, inc=1, device_id={"mlp": peer(k)}, device_id_type=MESH)
    for k in range(1, X):
        pl.semaphore_signal(barrier, inc=1, device_id={"req": rpeer(k)}, device_id_type=MESH)
    for copy in mine:
        copy.wait()
    pl.semaphore_wait(barrier, A + X)

    started = []

    def send(copy):
        copy.start()
        started.append(copy)

    def spread(slot, send_sem, recv_sem):
        src = slot(me)
        for k in range(1, A):
            send(remote(src, slot(me), send_sem.at[k], recv_sem.at[me], "mlp", peer(k)))
        send(remote(src, slot(me), send_sem.at[0], recv_sem.at[me], "mlp", partner))

    def arrived(slot, s, recv_sem, send_sem):
        remote(slot(s), slot(s), send_sem.at[0], recv_sem.at[s], "mlp", partner).wait_recv()

    def forward(k, slot, recv_sem, fwd_sem):
        s = peer(k)
        arrived(slot, s, recv_sem, fwd_sem)
        send(remote(slot(s), slot(s), fwd_sem.at[k], recv_sem.at[s], "mlp", partner))

    def other(k):
        return flip(a, k) * 2 + 1 - b

    spread(kv_slot, kv_send, kv_recv)
    for i in range(3):
        for k in range(1, X):
            send(remote(weights[i], w_slot(i, r), w_send.at[i, k], w_recv.at[i, r], "req", rpeer(k)))
    for i in range(3):
        send(remote(weights[i], w_slot(i, r), w_send.at[i, 0], w_recv.at[i, r], "req", sibling))
    own_ow.start()
    for copy in own_w:
        copy.start()

    def forward_weight(i):
        for k in range(1, X):
            s = rpeer(k)
            remote(w_slot(i, s), w_slot(i, s), w_fwd.at[i, k], w_recv.at[i, s], "req", sibling).wait_recv()
            send(remote(w_slot(i, s), w_slot(i, s), w_fwd.at[i, k], w_recv.at[i, s], "req", sibling))

    def weight_arrived(i):
        own_w[i].wait()
        for k in range(X):
            s = flip(x, k) * 2 + 1 - c
            remote(w_slot(i, s), w_slot(i, s), w_fwd.at[i, 0], w_recv.at[i, s], "req", sibling).wait_recv()

    rows = lax.broadcasted_iota(jnp.int32, (T, n * R), 0) + me * T
    bias[...] = jnp.where(pos_ref[...] <= rows, 0.0, -1e30)
    for k in range(1, A):
        forward(k, kv_slot, kv_recv, kv_fwd)
    for k in range(A):
        arrived(kv_slot, other(k), kv_recv, kv_fwd)

    factor = HEAD_SIZE ** (-0.5) * math.log2(math.e)

    def attend(i, carry):
        head = 2 * i
        g = head // GROUP
        first = pl.multiple_of(head * HEAD_SIZE, 128)
        second = pl.multiple_of(head * HEAD_SIZE + HEAD_SIZE, 128)
        qq = jnp.concatenate(
            [q_ref[:, pl.ds(first, HEAD_SIZE)], q_ref[:, pl.ds(second, HEAD_SIZE)]], axis=0
        )
        keys = kv[:, pl.ds(pl.multiple_of(g * HEAD_SIZE, 128), HEAD_SIZE)]
        values = kv[:, pl.ds(pl.multiple_of(KV_COLS + g * HEAD_SIZE, 128), HEAD_SIZE)]
        s = lax.dot_general(qq, keys, (((1,), (1,)), ((), ())), preferred_element_type=jnp.float32)
        s = (s * factor).reshape(2, T, n * R) + bias[...][None]
        e = jnp.exp2(s - jnp.max(s, axis=-1, keepdims=True))
        total = jnp.sum(e, axis=-1, keepdims=True)
        o = jnp.dot(
            e.astype(jnp.bfloat16).reshape(2 * T, n * R), values, preferred_element_type=jnp.float32
        ).reshape(2, T, HEAD_SIZE) / total
        attn[:, pl.ds(first, HEAD_SIZE)] = o[0].astype(jnp.bfloat16)
        attn[:, pl.ds(second, HEAD_SIZE)] = o[1].astype(jnp.bfloat16)
        return carry

    lax.fori_loop(0, QUERY_HEADS // 2, attend, 0)

    own_ow.wait()

    def project(j, squares):
        cols = pl.ds(pl.multiple_of(j * 256, 256), 256)
        piece = resid_ref[:, cols].astype(jnp.float32) + jnp.dot(
            attn[...], big[pl.ds(0, QUERY_HEADS * HEAD_SIZE), cols], preferred_element_type=jnp.float32
        )
        h[:, cols] = piece
        return squares + jnp.sum(piece * piece, axis=-1, keepdims=True)

    squares = lax.fori_loop(0, D // 256, project, jnp.zeros((T, 1), jnp.float32))
    inverse = lax.rsqrt(squares / D + 1e-05)
    nrm[pl.ds(pl.multiple_of(me * T, 128), T), :] = (h[...] * inverse * gain_ref[...]).astype(jnp.bfloat16)
    spread(n_slot, n_send, n_recv)

    width = 256 if Dq % 256 == 0 else 128

    def feed(ap):
        pair = pl.ds(pl.multiple_of(ap * 2 * T, 256), 2 * T)

        def gated(j, carry):
            cols = pl.ds(pl.multiple_of(j * 256, 256), 256)
            gate = jnp.dot(nrm[pair, :], wgs[:, cols], preferred_element_type=jnp.float32)
            upper = jnp.dot(nrm[pair, :], wus[:, cols], preferred_element_type=jnp.float32)
            hid[:, cols] = (gate / (1.0 + jnp.exp(-gate)) * upper).astype(jnp.bfloat16)
            return carry

        lax.fori_loop(0, F // 256, gated, 0)

        def lowered(s, carry):
            for j in range(Dq // width):
                piece = jnp.dot(
                    hid[...], wds[s, :, j * width : (j + 1) * width], preferred_element_type=jnp.float32
                )
                cols = pl.ds(pl.multiple_of(s * Dq + j * width, 128), width)
                big[pair, cols] = piece.astype(jnp.bfloat16)
            return carry

        lax.fori_loop(0, nr, lowered, 0)

    def p_slot(s):
        return pl.ds(pl.multiple_of(s * T, 128), T)

    def y_copy(k):
        return remote(big.at[p_slot(other(k)), :], yrecv.at[k], y_send.at[k], y_recv.at[k], "mlp", partner)

    def z_copy(k):
        return remote(big.at[p_slot(peer(k)), :], zrecv.at[k - 1], z_send.at[k], z_recv.at[k], "mlp", peer(k))

    def combine(k):
        y_copy(k).wait_recv()
        rows = p_slot(peer(k))
        big[rows, :] = (big[rows, :].astype(jnp.float32) + yrecv[k].astype(jnp.float32)).astype(jnp.bfloat16)
        send(z_copy(k))

    forward_weight(0)
    forward_weight(1)
    if A > 1:
        forward(1, n_slot, n_recv, n_fwd)
    forward_weight(2)
    for i in range(3):
        weight_arrived(i)
    for k in range(A):
        arrived(n_slot, other(k), n_recv, n_fwd)
        feed(flip(a, k))
        send(y_copy(k))
        if k + 2 < A:
            forward(k + 2, n_slot, n_recv, n_fwd)
        if k >= 2:
            combine(k - 1)
    if A > 1:
        combine(A - 1)
    y_copy(0).wait_recv()
    h[...] = h[...] + (big[p_slot(me), :].astype(jnp.float32) + yrecv[0].astype(jnp.float32))
    for k in range(1, A):
        z_copy(k).wait_recv()
        h[...] = h[...] + zrecv[k - 1].astype(jnp.float32)
    out_ref[...] = h[...].astype(jnp.bfloat16)
    for copy in started:
        copy.wait_send()


def body(
    n, nr,
    resid, queries, fresh_keys, fresh_values, paged_key_cache, paged_value_cache,
    page_table, cache_lengths, out_weight, norm_gain, gate_weight, up_weight, down_weight,
):
    T, D = resid.shape
    own_pages, page_tokens = paged_key_cache.shape[:2]
    cached = own_pages * page_tokens
    R = cached + T
    A, X = n // 2, nr // 2
    slots = jnp.arange(n * own_pages, dtype=jnp.int32)
    match = page_table[0][None, :] == slots[:, None]
    page = jnp.sum(jnp.where(match, jnp.arange(page_table.shape[1], dtype=jnp.int32)[None, :], 0), axis=1)
    positions = page[:, None] * page_tokens + jnp.arange(page_tokens, dtype=jnp.int32)[None, :]
    live = jnp.any(match, axis=1)[:, None] & (positions < cache_lengths[0])
    stored = jnp.where(live, -1, 2**30).reshape(n, cached)
    fresh = jnp.arange(n * T, dtype=jnp.int32).reshape(n, T)
    pos = jnp.concatenate([stored, fresh], axis=1).reshape(1, n * R)
    depth, F = gate_weight.shape
    Dq = down_weight.shape[1]
    bf16, f32 = jnp.bfloat16, jnp.float32
    dma = pltpu.SemaphoreType.DMA
    vmem = pl.BlockSpec(memory_space=pltpu.VMEM)
    hbm = pl.BlockSpec(memory_space=pl.ANY)
    return pl.pallas_call(
        functools.partial(kernel, n, nr),
        out_shape=jax.ShapeDtypeStruct((T, D), bf16),
        in_specs=[vmem] * 4 + [hbm] * 8,
        out_specs=vmem,
        scratch_shapes=[
            pltpu.VMEM((n * R, 2 * KV_COLS), bf16),
            pltpu.VMEM((n * T, D), bf16),
            pltpu.VMEM((nr * depth, F), bf16),
            pltpu.VMEM((nr * depth, F), bf16),
            pltpu.VMEM((nr, F, Dq), bf16),
            pltpu.VMEM((max(n * T, out_weight.shape[0]), D), bf16),
            pltpu.VMEM((A, T, D), bf16),
            pltpu.VMEM((A - 1, T, D), bf16),
            pltpu.VMEM((T, D), f32),
            pltpu.VMEM((T, QUERY_HEADS * HEAD_SIZE), bf16),
            pltpu.VMEM((T, n * R), f32),
            pltpu.VMEM((2 * T, F), bf16),
            dma((8,)),
            dma((A,)), dma((A,)), dma((n,)),
            dma((A,)), dma((A,)), dma((n,)),
            dma((3, X)), dma((3, X)), dma((3, nr)),
            dma((A,)), dma((A,)), dma((A,)), dma((A,)),
        ],
        compiler_params=pltpu.CompilerParams(
            collective_id=0, has_side_effects=True, vmem_limit_bytes=62 * 2**20
        ),
    )(
        queries, resid, pos, norm_gain.reshape(1, D), fresh_keys, fresh_values,
        paged_key_cache.reshape(cached, KV_COLS), paged_value_cache.reshape(cached, KV_COLS),
        out_weight, gate_weight, up_weight, down_weight,
    )


def solution(mesh):
    placed = (
        P(("req", "mlp"), None),
        P(("req", "mlp"), None),
        P(("req", "mlp"), None),
        P(("req", "mlp"), None),
        P(("req", "mlp"), None, None),
        P(("req", "mlp"), None, None),
        P("req", None),
        P("req"),
        P(),
        P(),
        P("req", "mlp"),
        P("req", "mlp"),
        P("mlp", "req"),
    )
    return jax.shard_map(
        functools.partial(body, mesh.shape["mlp"], mesh.shape["req"]),
        mesh=mesh, in_specs=placed, out_specs=P(("req", "mlp"), None), check_vma=False,
    )
```

```python
import functools
import math

import jax
import jax.numpy as jnp
from jax import lax
from jax.experimental import pallas as pl
from jax.experimental.pallas import tpu as pltpu
from jax.sharding import PartitionSpec as P

QUERY_HEADS = 12
KEY_VALUE_HEADS = 2
HEAD_SIZE = 128
GROUP = QUERY_HEADS // KEY_VALUE_HEADS
KV_COLS = KEY_VALUE_HEADS * HEAD_SIZE
MESH = pl.DeviceIdType.MESH


def flip(a, k):
    bit = 1
    while bit <= k:
        if k & bit:
            a = a + bit - 2 * bit * (lax.rem(a // bit, 2))
        bit *= 2
    return a


def at_least(u, v):
    return (u - v + 1024) // 1024


def nearest(a, count, j):
    if j == 0:
        return a
    low = 1 - at_least(a, count // 2)
    room = low * a + (1 - low) * (count - 1 - a)
    both = at_least(2 * room, j)
    step = (j + 1) // 2
    return a + both * (-step if j % 2 else step) + (1 - both) * (2 * low - 1) * (j - room)


def kernel(
    n, nr,
    q_ref, resid_ref, pos_ref, gain_ref, fk, fv, pk, pv, ow, wg, wu, wd,
    out_ref,
    kv, nrm, wgs, wus, wds, big, yrecv, zrecv, h, attn, bias, hid,
    loc, kv_send, kv_line, kv_recv, n_send, n_line, n_recv,
    w_send, w_fwd, w_recv, y_send, y_recv, z_send, z_recv,
):
    A, X = n // 2, nr // 2
    me, r = lax.axis_index("mlp"), lax.axis_index("req")
    a, b = me // 2, lax.rem(me, 2)
    x, c = r // 2, lax.rem(r, 2)
    partner, sibling = a * 2 + 1 - b, x * 2 + 1 - c
    T, D = resid_ref.shape
    cached = pk.shape[0]
    R = cached + T
    depth = wg.shape[0]
    F = wg.shape[1]
    Dq = wd.shape[1]

    def peer(k):
        return nearest(a, A, k) * 2 + b

    def rpeer(k):
        return flip(x, k) * 2 + c

    def remote(src, dst, ss, rs, axis, idx):
        return pltpu.make_async_remote_copy(
            src_ref=src, dst_ref=dst, send_sem=ss, recv_sem=rs,
            device_id={axis: idx}, device_id_type=MESH,
        )

    def kv_slot(s):
        return kv.at[pl.ds(pl.multiple_of(s * R, 128), R), :]

    def n_slot(s):
        return nrm.at[pl.ds(pl.multiple_of(s * T, 128), T), :]

    def w_slot(i, s):
        if i == 2:
            return wds.at[s]
        buf = wgs if i == 0 else wus
        return buf.at[pl.ds(pl.multiple_of(s * depth, 128), depth), :]

    weights = (wg, wu, wd)

    base = pl.multiple_of(me * R, 128)
    mine = [
        pltpu.make_async_copy(pk, kv.at[pl.ds(base, cached), pl.ds(0, KV_COLS)], loc.at[0]),
        pltpu.make_async_copy(pv, kv.at[pl.ds(base, cached), pl.ds(KV_COLS, KV_COLS)], loc.at[1]),
        pltpu.make_async_copy(fk, kv.at[pl.ds(base + cached, T), pl.ds(0, KV_COLS)], loc.at[2]),
        pltpu.make_async_copy(fv, kv.at[pl.ds(base + cached, T), pl.ds(KV_COLS, KV_COLS)], loc.at[3]),
    ]
    own_ow = pltpu.make_async_copy(ow, big.at[pl.ds(0, ow.shape[0]), :], loc.at[4])
    own_w = [pltpu.make_async_copy(weights[i], w_slot(i, r), loc.at[5 + i]) for i in range(3)]
    for copy in mine:
        copy.start()

    barrier = pltpu.get_barrier_semaphore()
    pl.semaphore_signal(barrier, inc=1, device_id={"mlp": partner}, device_id_type=MESH)
    pl.semaphore_signal(barrier, inc=1, device_id={"req": sibling}, device_id_type=MESH)
    for k in range(1, A):
        pl.semaphore_signal(barrier, inc=1, device_id={"mlp": peer(k)}, device_id_type=MESH)
    for k in range(1, X):
        pl.semaphore_signal(barrier, inc=1, device_id={"req": rpeer(k)}, device_id_type=MESH)
    for copy in mine:
        copy.wait()
    pl.semaphore_wait(barrier, A + X)

    started = []

    def send(copy, when=None):
        started.append((copy, when))
        if when is None:
            copy.start()
        else:
            pl.when(when)(copy.start)

    def along(slot, s, to, sem, recv_sem):
        copy = remote(slot(s), slot(s), sem, recv_sem.at[s], "mlp", to * 2 + b)
        send(copy, (to >= 0) & (to < A))

    def across(slot, s, sem, recv_sem):
        send(remote(slot(s), slot(s), sem, recv_sem.at[s], "mlp", partner))

    def spread(slot, send_sem, line_sem, recv_sem):
        along(slot, me, a + 1, line_sem.at[0], recv_sem)
        along(slot, me, a - 1, line_sem.at[A], recv_sem)
        across(slot, me, send_sem.at[0], recv_sem)

    def arrived(slot, s, recv_sem):
        remote(slot(s), slot(s), recv_sem.at[s], recv_sem.at[s], "mlp", partner).wait_recv()

    def forward(k, slot, send_sem, line_sem, recv_sem):
        s = peer(k)
        arrived(slot, s, recv_sem)
        right = at_least(a, nearest(a, A, k))
        along(slot, s, a + 2 * right - 1, line_sem.at[k], recv_sem)
        across(slot, s, send_sem.at[k], recv_sem)

    def other(k):
        return nearest(a, A, k) * 2 + 1 - b

    spread(kv_slot, kv_send, kv_line, kv_recv)
    for i in range(3):
        for k in range(1, X):
            send(remote(weights[i], w_slot(i, r), w_send.at[i, k], w_recv.at[i, r], "req", rpeer(k)))
    for i in range(3):
        send(remote(weights[i], w_slot(i, r), w_send.at[i, 0], w_recv.at[i, r], "req", sibling))
    own_ow.start()
    for copy in own_w:
        copy.start()

    def forward_weight(i):
        for k in range(1, X):
            s = rpeer(k)
            remote(w_slot(i, s), w_slot(i, s), w_fwd.at[i, k], w_recv.at[i, s], "req", sibling).wait_recv()
            send(remote(w_slot(i, s), w_slot(i, s), w_fwd.at[i, k], w_recv.at[i, s], "req", sibling))

    def weight_arrived(i):
        own_w[i].wait()
        for k in range(X):
            s = flip(x, k) * 2 + 1 - c
            remote(w_slot(i, s), w_slot(i, s), w_fwd.at[i, 0], w_recv.at[i, s], "req", sibling).wait_recv()

    rows = lax.broadcasted_iota(jnp.int32, (T, n * R), 0) + me * T
    bias[...] = jnp.where(pos_ref[...] <= rows, 0.0, -1e30)
    for k in range(1, A):
        forward(k, kv_slot, kv_send, kv_line, kv_recv)
    for k in range(A):
        arrived(kv_slot, other(k), kv_recv)

    factor = HEAD_SIZE ** (-0.5) * math.log2(math.e)

    def attend(i, carry):
        head = 2 * i
        g = head // GROUP
        first = pl.multiple_of(head * HEAD_SIZE, 128)
        second = pl.multiple_of(head * HEAD_SIZE + HEAD_SIZE, 128)
        qq = jnp.concatenate(
            [q_ref[:, pl.ds(first, HEAD_SIZE)], q_ref[:, pl.ds(second, HEAD_SIZE)]], axis=0
        )
        keys = kv[:, pl.ds(pl.multiple_of(g * HEAD_SIZE, 128), HEAD_SIZE)]
        values = kv[:, pl.ds(pl.multiple_of(KV_COLS + g * HEAD_SIZE, 128), HEAD_SIZE)]
        s = lax.dot_general(qq, keys, (((1,), (1,)), ((), ())), preferred_element_type=jnp.float32)
        s = (s * factor).reshape(2, T, n * R) + bias[...][None]
        e = jnp.exp2(s - jnp.max(s, axis=-1, keepdims=True))
        total = jnp.sum(e, axis=-1, keepdims=True)
        o = jnp.dot(
            e.astype(jnp.bfloat16).reshape(2 * T, n * R), values, preferred_element_type=jnp.float32
        ).reshape(2, T, HEAD_SIZE) / total
        attn[:, pl.ds(first, HEAD_SIZE)] = o[0].astype(jnp.bfloat16)
        attn[:, pl.ds(second, HEAD_SIZE)] = o[1].astype(jnp.bfloat16)
        return carry

    lax.fori_loop(0, QUERY_HEADS // 2, attend, 0)

    own_ow.wait()

    def project(j, squares):
        cols = pl.ds(pl.multiple_of(j * 256, 256), 256)
        piece = resid_ref[:, cols].astype(jnp.float32) + jnp.dot(
            attn[...], big[pl.ds(0, QUERY_HEADS * HEAD_SIZE), cols], preferred_element_type=jnp.float32
        )
        h[:, cols] = piece
        return squares + jnp.sum(piece * piece, axis=-1, keepdims=True)

    squares = lax.fori_loop(0, D // 256, project, jnp.zeros((T, 1), jnp.float32))
    inverse = lax.rsqrt(squares / D + 1e-05)
    nrm[pl.ds(pl.multiple_of(me * T, 128), T), :] = (h[...] * inverse * gain_ref[...]).astype(jnp.bfloat16)
    spread(n_slot, n_send, n_line, n_recv)

    width = 256 if Dq % 256 == 0 else 128

    def feed(ap):
        pair = pl.ds(pl.multiple_of(ap * 2 * T, 256), 2 * T)

        def gated(j, carry):
            cols = pl.ds(pl.multiple_of(j * 256, 256), 256)
            gate = jnp.dot(nrm[pair, :], wgs[:, cols], preferred_element_type=jnp.float32)
            upper = jnp.dot(nrm[pair, :], wus[:, cols], preferred_element_type=jnp.float32)
            hid[:, cols] = (gate / (1.0 + jnp.exp(-gate)) * upper).astype(jnp.bfloat16)
            return carry

        lax.fori_loop(0, F // 256, gated, 0)

        def lowered(s, carry):
            for j in range(Dq // width):
                piece = jnp.dot(
                    hid[...], wds[s, :, j * width : (j + 1) * width], preferred_element_type=jnp.float32
                )
                cols = pl.ds(pl.multiple_of(s * Dq + j * width, 128), width)
                big[pair, cols] = piece.astype(jnp.bfloat16)
            return carry

        lax.fori_loop(0, nr, lowered, 0)

    def p_slot(s):
        return pl.ds(pl.multiple_of(s * T, 128), T)

    def y_copy(k):
        return remote(big.at[p_slot(other(k)), :], yrecv.at[k], y_send.at[k], y_recv.at[k], "mlp", partner)

    def z_copy(k):
        return remote(big.at[p_slot(peer(k)), :], zrecv.at[a], z_send.at[k], z_recv.at[a], "mlp", peer(k))

    def combine(k):
        y_copy(k).wait_recv()
        rows = p_slot(peer(k))
        big[rows, :] = (big[rows, :].astype(jnp.float32) + yrecv[k].astype(jnp.float32)).astype(jnp.bfloat16)
        send(z_copy(k))

    for k in range(1, A - 1):
        forward(k, n_slot, n_send, n_line, n_recv)
    for i in range(3):
        forward_weight(i)
    if A > 1:
        forward(A - 1, n_slot, n_send, n_line, n_recv)
    for i in range(3):
        weight_arrived(i)
    order = [*range(1, A), 0]
    for i, k in enumerate(order):
        arrived(n_slot, other(k), n_recv)
        feed(nearest(a, A, k))
        send(y_copy(k))
        if i:
            combine(order[i - 1])
    y_copy(0).wait_recv()
    h[...] = h[...] + (big[p_slot(me), :].astype(jnp.float32) + yrecv[0].astype(jnp.float32))
    for k in range(1, A):
        s = nearest(a, A, k)
        remote(zrecv.at[s], zrecv.at[s], z_send.at[k], z_recv.at[s], "mlp", partner).wait_recv()
        h[...] = h[...] + zrecv[s].astype(jnp.float32)
    out_ref[...] = h[...].astype(jnp.bfloat16)
    for copy, when in started:
        if when is None:
            copy.wait_send()
        else:
            pl.when(when)(copy.wait_send)


def body(
    n, nr,
    resid, queries, fresh_keys, fresh_values, paged_key_cache, paged_value_cache,
    page_table, cache_lengths, out_weight, norm_gain, gate_weight, up_weight, down_weight,
):
    T, D = resid.shape
    own_pages, page_tokens = paged_key_cache.shape[:2]
    cached = own_pages * page_tokens
    R = cached + T
    A, X = n // 2, nr // 2
    slots = jnp.arange(n * own_pages, dtype=jnp.int32)
    match = page_table[0][None, :] == slots[:, None]
    page = jnp.sum(jnp.where(match, jnp.arange(page_table.shape[1], dtype=jnp.int32)[None, :], 0), axis=1)
    positions = page[:, None] * page_tokens + jnp.arange(page_tokens, dtype=jnp.int32)[None, :]
    live = jnp.any(match, axis=1)[:, None] & (positions < cache_lengths[0])
    stored = jnp.where(live, -1, 2**30).reshape(n, cached)
    fresh = jnp.arange(n * T, dtype=jnp.int32).reshape(n, T)
    pos = jnp.concatenate([stored, fresh], axis=1).reshape(1, n * R)
    depth, F = gate_weight.shape
    Dq = down_weight.shape[1]
    bf16, f32 = jnp.bfloat16, jnp.float32
    dma = pltpu.SemaphoreType.DMA
    vmem = pl.BlockSpec(memory_space=pltpu.VMEM)
    hbm = pl.BlockSpec(memory_space=pl.ANY)
    return pl.pallas_call(
        functools.partial(kernel, n, nr),
        out_shape=jax.ShapeDtypeStruct((T, D), bf16),
        in_specs=[vmem] * 4 + [hbm] * 8,
        out_specs=vmem,
        scratch_shapes=[
            pltpu.VMEM((n * R, 2 * KV_COLS), bf16),
            pltpu.VMEM((n * T, D), bf16),
            pltpu.VMEM((nr * depth, F), bf16),
            pltpu.VMEM((nr * depth, F), bf16),
            pltpu.VMEM((nr, F, Dq), bf16),
            pltpu.VMEM((max(n * T, out_weight.shape[0]), D), bf16),
            pltpu.VMEM((A, T, D), bf16),
            pltpu.VMEM((A, T, D), bf16),
            pltpu.VMEM((T, D), f32),
            pltpu.VMEM((T, QUERY_HEADS * HEAD_SIZE), bf16),
            pltpu.VMEM((T, n * R), f32),
            pltpu.VMEM((2 * T, F), bf16),
            dma((8,)),
            dma((A,)), dma((A + 1,)), dma((n,)),
            dma((A,)), dma((A + 1,)), dma((n,)),
            dma((3, X)), dma((3, X)), dma((3, nr)),
            dma((A,)), dma((A,)), dma((A,)), dma((A,)),
        ],
        compiler_params=pltpu.CompilerParams(
            collective_id=0, has_side_effects=True, vmem_limit_bytes=62 * 2**20
        ),
    )(
        queries, resid, pos, norm_gain.reshape(1, D), fresh_keys, fresh_values,
        paged_key_cache.reshape(cached, KV_COLS), paged_value_cache.reshape(cached, KV_COLS),
        out_weight, gate_weight, up_weight, down_weight,
    )


def solution(mesh):
    placed = (
        P(("req", "mlp"), None),
        P(("req", "mlp"), None),
        P(("req", "mlp"), None),
        P(("req", "mlp"), None),
        P(("req", "mlp"), None, None),
        P(("req", "mlp"), None, None),
        P("req", None),
        P("req"),
        P(),
        P(),
        P("req", "mlp"),
        P("req", "mlp"),
        P("mlp", "req"),
    )
    return jax.shard_map(
        functools.partial(body, mesh.shape["mlp"], mesh.shape["req"]),
        mesh=mesh, in_specs=placed, out_specs=P(("req", "mlp"), None), check_vma=False,
    )
```

```python
import functools
import math

import jax
import jax.numpy as jnp
from jax import lax
from jax.experimental import pallas as pl
from jax.experimental.pallas import tpu as pltpu
from jax.sharding import PartitionSpec as P

QUERY_HEADS = 12
KEY_VALUE_HEADS = 2
HEAD_SIZE = 128
GROUP = QUERY_HEADS // KEY_VALUE_HEADS
KV_COLS = KEY_VALUE_HEADS * HEAD_SIZE
MESH = pl.DeviceIdType.MESH


def flip(a, k):
    bit = 1
    while bit <= k:
        if k & bit:
            a = a + bit - 2 * bit * (lax.rem(a // bit, 2))
        bit *= 2
    return a


def at_least(u, v):
    return (u - v + 1024) // 1024


def nearest(a, count, j):
    if j == 0:
        return a
    low = 1 - at_least(a, count // 2)
    room = low * a + (1 - low) * (count - 1 - a)
    both = at_least(2 * room, j)
    step = (j + 1) // 2
    return a + both * (-step if j % 2 else step) + (1 - both) * (2 * low - 1) * (j - room)


def kernel(
    n, nr,
    q_ref, resid_ref, pos_ref, gain_ref, fk, fv, pk, pv, ow, wg, wu, wd,
    out_ref,
    kv, nrm, wgs, wus, wds, big, yrecv, zrecv, h, attn, bias, hid,
    loc, kv_send, kv_line, kv_recv, n_send, n_line, n_recv,
    w_send, w_fwd, w_recv, y_send, y_recv, z_send, z_recv,
):
    A, X = n // 2, nr // 2
    me, r = lax.axis_index("mlp"), lax.axis_index("req")
    a, b = me // 2, lax.rem(me, 2)
    x, c = r // 2, lax.rem(r, 2)
    partner, sibling = a * 2 + 1 - b, x * 2 + 1 - c
    T, D = resid_ref.shape
    cached = pk.shape[0]
    R = cached + T
    depth = wg.shape[0]
    F = wg.shape[1]
    Dq = wd.shape[1]

    def peer(k):
        return nearest(a, A, k) * 2 + b

    def rpeer(k):
        return flip(x, k) * 2 + c

    def remote(src, dst, ss, rs, axis, idx):
        return pltpu.make_async_remote_copy(
            src_ref=src, dst_ref=dst, send_sem=ss, recv_sem=rs,
            device_id={axis: idx}, device_id_type=MESH,
        )

    def kv_slot(s):
        return kv.at[pl.ds(pl.multiple_of(s * R, 128), R), :]

    def n_slot(s):
        return nrm.at[pl.ds(pl.multiple_of(s * T, 128), T), :]

    def w_slot(i, s):
        if i == 2:
            return wds.at[s]
        buf = wgs if i == 0 else wus
        return buf.at[pl.ds(pl.multiple_of(s * depth, 128), depth), :]

    weights = (wg, wu, wd)

    base = pl.multiple_of(me * R, 128)
    mine = [
        pltpu.make_async_copy(pk, kv.at[pl.ds(base, cached), pl.ds(0, KV_COLS)], loc.at[0]),
        pltpu.make_async_copy(pv, kv.at[pl.ds(base, cached), pl.ds(KV_COLS, KV_COLS)], loc.at[1]),
        pltpu.make_async_copy(fk, kv.at[pl.ds(base + cached, T), pl.ds(0, KV_COLS)], loc.at[2]),
        pltpu.make_async_copy(fv, kv.at[pl.ds(base + cached, T), pl.ds(KV_COLS, KV_COLS)], loc.at[3]),
    ]
    own_ow = pltpu.make_async_copy(ow, big.at[pl.ds(0, ow.shape[0]), :], loc.at[4])
    own_w = [pltpu.make_async_copy(weights[i], w_slot(i, r), loc.at[5 + i]) for i in range(3)]
    for copy in mine:
        copy.start()

    barrier = pltpu.get_barrier_semaphore()
    pl.semaphore_signal(barrier, inc=1, device_id={"mlp": partner}, device_id_type=MESH)
    pl.semaphore_signal(barrier, inc=1, device_id={"req": sibling}, device_id_type=MESH)
    for k in range(1, A):
        pl.semaphore_signal(barrier, inc=1, device_id={"mlp": peer(k)}, device_id_type=MESH)
    for k in range(1, X):
        pl.semaphore_signal(barrier, inc=1, device_id={"req": rpeer(k)}, device_id_type=MESH)
    for copy in mine:
        copy.wait()
    pl.semaphore_wait(barrier, A + X)

    started = []

    def send(copy, when=None):
        started.append((copy, when))
        if when is None:
            copy.start()
        else:
            pl.when(when)(copy.start)

    def along(slot, s, to, sem, recv_sem):
        copy = remote(slot(s), slot(s), sem, recv_sem.at[s], "mlp", to * 2 + b)
        send(copy, (to >= 0) & (to < A))

    def across(slot, s, sem, recv_sem):
        send(remote(slot(s), slot(s), sem, recv_sem.at[s], "mlp", partner))

    def spread(slot, send_sem, line_sem, recv_sem):
        along(slot, me, a + 1, line_sem.at[0], recv_sem)
        along(slot, me, a - 1, line_sem.at[A], recv_sem)
        across(slot, me, send_sem.at[0], recv_sem)

    def arrived(slot, s, recv_sem):
        remote(slot(s), slot(s), recv_sem.at[s], recv_sem.at[s], "mlp", partner).wait_recv()

    def forward(k, slot, send_sem, line_sem, recv_sem):
        s = peer(k)
        arrived(slot, s, recv_sem)
        right = at_least(a, nearest(a, A, k))
        along(slot, s, a + 2 * right - 1, line_sem.at[k], recv_sem)
        across(slot, s, send_sem.at[k], recv_sem)

    def other(k):
        return nearest(a, A, k) * 2 + 1 - b

    spread(kv_slot, kv_send, kv_line, kv_recv)
    def weight_out(i):
        for k in range(1, X):
            send(remote(weights[i], w_slot(i, r), w_send.at[i, k], w_recv.at[i, r], "req", rpeer(k)))

    weight_out(0)
    weight_out(1)
    for i in range(3):
        send(remote(weights[i], w_slot(i, r), w_send.at[i, 0], w_recv.at[i, r], "req", sibling))
    own_ow.start()
    for copy in own_w:
        copy.start()

    def forward_weight(i):
        for k in range(1, X):
            s = rpeer(k)
            remote(w_slot(i, s), w_slot(i, s), w_fwd.at[i, k], w_recv.at[i, s], "req", sibling).wait_recv()
            send(remote(w_slot(i, s), w_slot(i, s), w_fwd.at[i, k], w_recv.at[i, s], "req", sibling))

    def weight_arrived(i):
        own_w[i].wait()
        for k in range(X):
            s = flip(x, k) * 2 + 1 - c
            remote(w_slot(i, s), w_slot(i, s), w_fwd.at[i, 0], w_recv.at[i, s], "req", sibling).wait_recv()

    rows = lax.broadcasted_iota(jnp.int32, (T, n * R), 0) + me * T
    bias[...] = jnp.where(pos_ref[...] <= rows, 0.0, -1e30)
    for k in range(1, A):
        forward(k, kv_slot, kv_send, kv_line, kv_recv)
    for k in range(A):
        arrived(kv_slot, other(k), kv_recv)
    weight_out(2)

    factor = HEAD_SIZE ** (-0.5) * math.log2(math.e)

    def attend(i, carry):
        head = 2 * i
        g = head // GROUP
        first = pl.multiple_of(head * HEAD_SIZE, 128)
        second = pl.multiple_of(head * HEAD_SIZE + HEAD_SIZE, 128)
        qq = jnp.concatenate(
            [q_ref[:, pl.ds(first, HEAD_SIZE)], q_ref[:, pl.ds(second, HEAD_SIZE)]], axis=0
        )
        keys = kv[:, pl.ds(pl.multiple_of(g * HEAD_SIZE, 128), HEAD_SIZE)]
        values = kv[:, pl.ds(pl.multiple_of(KV_COLS + g * HEAD_SIZE, 128), HEAD_SIZE)]
        s = lax.dot_general(qq, keys, (((1,), (1,)), ((), ())), preferred_element_type=jnp.float32)
        s = (s * factor).reshape(2, T, n * R) + bias[...][None]
        e = jnp.exp2(s - jnp.max(s, axis=-1, keepdims=True))
        total = jnp.sum(e, axis=-1, keepdims=True)
        o = jnp.dot(
            e.astype(jnp.bfloat16).reshape(2 * T, n * R), values, preferred_element_type=jnp.float32
        ).reshape(2, T, HEAD_SIZE) / total
        attn[:, pl.ds(first, HEAD_SIZE)] = o[0].astype(jnp.bfloat16)
        attn[:, pl.ds(second, HEAD_SIZE)] = o[1].astype(jnp.bfloat16)
        return carry

    lax.fori_loop(0, QUERY_HEADS // 2, attend, 0)

    own_ow.wait()

    def project(j, squares):
        cols = pl.ds(pl.multiple_of(j * 256, 256), 256)
        piece = resid_ref[:, cols].astype(jnp.float32) + jnp.dot(
            attn[...], big[pl.ds(0, QUERY_HEADS * HEAD_SIZE), cols], preferred_element_type=jnp.float32
        )
        h[:, cols] = piece
        return squares + jnp.sum(piece * piece, axis=-1, keepdims=True)

    squares = lax.fori_loop(0, D // 256, project, jnp.zeros((T, 1), jnp.float32))
    inverse = lax.rsqrt(squares / D + 1e-05)
    nrm[pl.ds(pl.multiple_of(me * T, 128), T), :] = (h[...] * inverse * gain_ref[...]).astype(jnp.bfloat16)
    spread(n_slot, n_send, n_line, n_recv)

    width = 256 if Dq % 256 == 0 else 128

    def feed(ap, wait, out):
        pair = pl.ds(pl.multiple_of(ap * 2 * T, 256), 2 * T)

        def gated(j, carry):
            cols = pl.ds(pl.multiple_of(j * 256, 256), 256)
            gate = jnp.dot(nrm[pair, :], wgs[:, cols], preferred_element_type=jnp.float32)
            upper = jnp.dot(nrm[pair, :], wus[:, cols], preferred_element_type=jnp.float32)
            hid[:, cols] = (gate / (1.0 + jnp.exp(-gate)) * upper).astype(jnp.bfloat16)
            return carry

        if wait:
            weight_arrived(0)
            weight_arrived(1)
        lax.fori_loop(0, F // 256, gated, 0)
        if wait:
            weight_arrived(2)

        def lowered(s, carry):
            for j in range(Dq // width):
                piece = jnp.dot(
                    hid[...], wds[s, :, j * width : (j + 1) * width], preferred_element_type=jnp.float32
                )
                cols = pl.ds(pl.multiple_of(s * Dq + j * width, 128), width)
                big[pair, cols] = piece.astype(jnp.bfloat16)
            return carry

        lax.fori_loop(0, nr // 2, lowered, 0)
        out(0)
        lax.fori_loop(nr // 2, nr, lowered, 0)
        out(1)

    def p_slot(s):
        return pl.ds(pl.multiple_of(s * T, 128), T)

    halves = (pl.ds(0, D // 2), pl.ds(D // 2, D // 2))

    def y_copy(k, f):
        return remote(
            big.at[p_slot(other(k)), halves[f]], yrecv.at[k, :, halves[f]],
            y_send.at[k, f], y_recv.at[k, f], "mlp", partner,
        )

    def z_copy(k, f):
        return remote(
            big.at[p_slot(peer(k)), halves[f]], zrecv.at[a, :, halves[f]],
            z_send.at[k, f], z_recv.at[a, f], "mlp", peer(k),
        )

    def combine(k):
        rows = p_slot(peer(k))
        for f, cols in enumerate(halves):
            y_copy(k, f).wait_recv()
            big[rows, cols] = (
                big[rows, cols].astype(jnp.float32) + yrecv[k, :, cols].astype(jnp.float32)
            ).astype(jnp.bfloat16)
            send(z_copy(k, f))

    for k in range(1, A - 1):
        forward(k, n_slot, n_send, n_line, n_recv)
    for i in range(3):
        forward_weight(i)
    if A > 1:
        forward(A - 1, n_slot, n_send, n_line, n_recv)
    order = [*range(A - 1, 0, -1), 0]
    for i, k in enumerate(order):
        arrived(n_slot, other(k), n_recv)
        feed(nearest(a, A, k), i == 0, lambda f: send(y_copy(k, f)))
        if i:
            combine(order[i - 1])
    for f, cols in enumerate(halves):
        y_copy(0, f).wait_recv()
        h[:, cols] = h[:, cols] + (
            big[p_slot(me), cols].astype(jnp.float32) + yrecv[0, :, cols].astype(jnp.float32)
        )
    for k in order[:-1]:
        s = nearest(a, A, k)
        for f, cols in enumerate(halves):
            here = zrecv.at[s, :, cols]
            remote(here, here, z_send.at[k, f], z_recv.at[s, f], "mlp", partner).wait_recv()
            h[:, cols] = h[:, cols] + zrecv[s, :, cols].astype(jnp.float32)
    out_ref[...] = h[...].astype(jnp.bfloat16)
    for copy, when in started:
        if when is None:
            copy.wait_send()
        else:
            pl.when(when)(copy.wait_send)


def body(
    n, nr,
    resid, queries, fresh_keys, fresh_values, paged_key_cache, paged_value_cache,
    page_table, cache_lengths, out_weight, norm_gain, gate_weight, up_weight, down_weight,
):
    T, D = resid.shape
    own_pages, page_tokens = paged_key_cache.shape[:2]
    cached = own_pages * page_tokens
    R = cached + T
    A, X = n // 2, nr // 2
    slots = jnp.arange(n * own_pages, dtype=jnp.int32)
    match = page_table[0][None, :] == slots[:, None]
    page = jnp.sum(jnp.where(match, jnp.arange(page_table.shape[1], dtype=jnp.int32)[None, :], 0), axis=1)
    positions = page[:, None] * page_tokens + jnp.arange(page_tokens, dtype=jnp.int32)[None, :]
    live = jnp.any(match, axis=1)[:, None] & (positions < cache_lengths[0])
    stored = jnp.where(live, -1, 2**30).reshape(n, cached)
    fresh = jnp.arange(n * T, dtype=jnp.int32).reshape(n, T)
    pos = jnp.concatenate([stored, fresh], axis=1).reshape(1, n * R)
    depth, F = gate_weight.shape
    Dq = down_weight.shape[1]
    bf16, f32 = jnp.bfloat16, jnp.float32
    dma = pltpu.SemaphoreType.DMA
    vmem = pl.BlockSpec(memory_space=pltpu.VMEM)
    hbm = pl.BlockSpec(memory_space=pl.ANY)
    return pl.pallas_call(
        functools.partial(kernel, n, nr),
        out_shape=jax.ShapeDtypeStruct((T, D), bf16),
        in_specs=[vmem] * 4 + [hbm] * 8,
        out_specs=vmem,
        scratch_shapes=[
            pltpu.VMEM((n * R, 2 * KV_COLS), bf16),
            pltpu.VMEM((n * T, D), bf16),
            pltpu.VMEM((nr * depth, F), bf16),
            pltpu.VMEM((nr * depth, F), bf16),
            pltpu.VMEM((nr, F, Dq), bf16),
            pltpu.VMEM((max(n * T, out_weight.shape[0]), D), bf16),
            pltpu.VMEM((A, T, D), bf16),
            pltpu.VMEM((A, T, D), bf16),
            pltpu.VMEM((T, D), f32),
            pltpu.VMEM((T, QUERY_HEADS * HEAD_SIZE), bf16),
            pltpu.VMEM((T, n * R), f32),
            pltpu.VMEM((2 * T, F), bf16),
            dma((8,)),
            dma((A,)), dma((A + 1,)), dma((n,)),
            dma((A,)), dma((A + 1,)), dma((n,)),
            dma((3, X)), dma((3, X)), dma((3, nr)),
            dma((A, 2)), dma((A, 2)), dma((A, 2)), dma((A, 2)),
        ],
        compiler_params=pltpu.CompilerParams(
            collective_id=0, has_side_effects=True, vmem_limit_bytes=62 * 2**20
        ),
    )(
        queries, resid, pos, norm_gain.reshape(1, D), fresh_keys, fresh_values,
        paged_key_cache.reshape(cached, KV_COLS), paged_value_cache.reshape(cached, KV_COLS),
        out_weight, gate_weight, up_weight, down_weight,
    )


def solution(mesh):
    placed = (
        P(("req", "mlp"), None),
        P(("req", "mlp"), None),
        P(("req", "mlp"), None),
        P(("req", "mlp"), None),
        P(("req", "mlp"), None, None),
        P(("req", "mlp"), None, None),
        P("req", None),
        P("req"),
        P(),
        P(),
        P("req", "mlp"),
        P("req", "mlp"),
        P("mlp", "req"),
    )
    return jax.shard_map(
        functools.partial(body, mesh.shape["mlp"], mesh.shape["req"]),
        mesh=mesh, in_specs=placed, out_specs=P(("req", "mlp"), None), check_vma=False,
    )
```
